32 devices in a mesh: ctx: 8 (over z, y), head: 4 (over x, core).
Axes of the slice: x: 2, y: 2, z: 4, core: 2. Of those that a mesh axis runs over, the one named last changes fastest.
Arguments:
- query_act: bfloat16 [2048, 4096], P('ctx', 'head'), may hold values from -6 to 6
- key_act: bfloat16 [2048, 4096], P('ctx', 'head'), may hold values from -6 to 6
- value_act: bfloat16 [2048, 4096], P('ctx', 'head'), may hold values from -6 to 6
- out_weight: bfloat16 [3072, 4096], P('ctx', 'head'), may hold values from -0.09375 to 0.09375
- out_cotangent: bfloat16 [2048, 3072], P('ctx', 'head'), may hold values from -6 to 6
Outputs:
- grad_query: bfloat16 [2048, 4096], P('ctx', 'head')
- grad_key: bfloat16 [2048, 4096], P('ctx', 'head')
- grad_value: bfloat16 [2048, 4096], P('ctx', 'head')
- grad_weight: float32 [3072, 4096], P('ctx', 'head')
The draws below stay inside these ranges and needn't reach their ends.
All inputs are finite; a program needn't handle non-finite values.
Results may differ from the reference program's by a relative error of at most 0.014.
Values may be sent and summed in bfloat16 or wider, within the bound.
No kernel may reach another device: no remote copies, remote signals or barrier semaphores. Data moves between devices by JAX's collectives and lax.ppermute only.
A program may use at most 128 MiB of HBM per device.

```python
import jax
import jax.numpy as jnp
from jax import lax

D = 3072
HDIM = 128
HEADS = 32
BLK = 256
TOKENS = 2048


def with_spikes(drawn, key, source, target, blocks, factor):
    owner, partner = [(jnp.arange(drawn.shape[position]) // (drawn.shape[position] // blocks)).reshape([-1 if axis == position else 1 for axis in range(drawn.ndim)]) for position in (source, target)]
    chosen = jax.random.permutation(key, blocks)[partner]
    strong = (owner == chosen) | (owner == (partner + blocks // 2) % blocks)
    return jnp.where(strong, factor * drawn, drawn)


def level_of(key, shape, split, smallest, high):
    level, own = 1.0, jax.random.fold_in(key, 6)
    for position, shards_of in split:
        heights = jnp.exp(jax.random.uniform(jax.random.fold_in(own, position), (shards_of,), jnp.float32, smallest / len(split), high / len(split)))
        level = level * jnp.repeat(heights, shape[position] // shards_of).reshape([-1 if axis == position else 1 for axis in range(len(shape))])
    return level


def centred(own_key, extent, spread, limit, cuts=(), held_as=jnp.bfloat16):
    array = jax.random.normal(own_key, extent, jnp.float32) * spread
    if len(cuts) > 0:
        array = level_of(own_key, extent, cuts, -0.22, 0.18) * array
    return jnp.clip(array, min=-limit, max=limit).astype(held_as)


def noise_with(key, extent, deviation, bound, split, heavy, held_as=jnp.bfloat16):
    values = deviation * jax.random.normal(key, extent, jnp.float32)
    if split:
        values = values * level_of(key, extent, split, -0.22, 0.18)
    return jnp.clip(with_spikes(values, jax.random.fold_in(key, 3), *heavy), -bound, bound).astype(held_as)


def setup_inputs(seed: int = 0) -> dict:
    arg_keys = jax.random.split(jax.random.key(seed), 6)
    return {
        "query_act": centred(arg_keys[0], (TOKENS, HEADS * HDIM), 1.0, 6.0, ((0, 8), (1, 4))),
        "key_act": centred(arg_keys[1], (TOKENS, HEADS * HDIM), 1.0, 6.0, ((0, 8), (1, 4))),
        "value_act": centred(arg_keys[2], (TOKENS, HEADS * HDIM), 1.0, 6.0, ((0, 8), (1, 4))),
        "out_weight": centred(arg_keys[3], (D, HEADS * HDIM), (HEADS * HDIM) ** -0.5, 0.09375, ((0, 8), (1, 4))),
        "out_cotangent": noise_with(arg_keys[4], (TOKENS, D), 1.0, 6.0, ((0, 8), (1, 4)), (0, 1, 8, 2.0)),
    }


EPS = 1e-06

def head_grads(pieces):
    q, k, v, da = pieces
    nb = TOKENS // BLK
    q = q.reshape(nb, BLK, HDIM).astype(jnp.float32)
    k = k.reshape(nb, BLK, HDIM).astype(jnp.float32)
    v = v.reshape(nb, BLK, HDIM).astype(jnp.float32)
    da = da.reshape(nb, BLK, HDIM)
    block_kv = jnp.einsum('bti,btj->bij', k, v)
    prior = (jnp.cumsum(block_kv, axis=0) - block_kv).astype(jnp.bfloat16).astype(jnp.float32)
    mask = jnp.tril(jnp.ones((BLK, BLK), jnp.float32))
    scores = (jnp.einsum('bti,bsi->bts', q, k) * mask).astype(jnp.bfloat16).astype(jnp.float32)
    raw = jnp.einsum('bts,bsj->btj', scores, v) + jnp.einsum('bti,bij->btj', q, prior)
    inv_rms = lax.rsqrt(lax.optimization_barrier(jnp.mean(raw * raw, axis=-1, keepdims=True)) + EPS)
    normal = raw * inv_rms
    normed = normal.astype(jnp.bfloat16)
    center = lax.optimization_barrier(jnp.mean(da * normal, axis=-1, keepdims=True))
    d_raw = (inv_rms * (da - normal * center)).astype(jnp.bfloat16).astype(jnp.float32)
    block_g = jnp.einsum('bti,btj->bij', q, d_raw)
    later = (lax.optimization_barrier(jnp.sum(block_g, axis=0)) - jnp.cumsum(block_g, axis=0)).astype(jnp.bfloat16).astype(jnp.float32)
    d_scores = (jnp.einsum('btj,bsj->bts', d_raw, v) * mask).astype(jnp.bfloat16).astype(jnp.float32)
    grad_q = jnp.einsum('bts,bsi->bti', d_scores, k) + jnp.einsum('btj,bij->bti', d_raw, prior)
    grad_k = jnp.einsum('bts,bti->bsi', d_scores, q) + jnp.einsum('bsj,bij->bsi', v, later)
    grad_v = jnp.einsum('bts,btj->bsj', scores, d_raw) + jnp.einsum('bsi,bij->bsj', k, later)
    shape = (TOKENS, HDIM)
    return (grad_q.reshape(shape).astype(jnp.bfloat16), grad_k.reshape(shape).astype(jnp.bfloat16), grad_v.reshape(shape).astype(jnp.bfloat16), normed.reshape(shape))

def by_head(x):
    return jnp.transpose(x.reshape(TOKENS, HEADS, HDIM), (1, 0, 2))

def back(x):
    return jnp.transpose(x, (1, 0, 2)).reshape(TOKENS, HEADS * HDIM)

def reference(query_act, key_act, value_act, out_weight, out_cotangent):
    d_attn = jnp.dot(out_cotangent, out_weight, preferred_element_type=jnp.float32)
    grad_q, grad_k, grad_v, normed = lax.map(head_grads, (by_head(query_act), by_head(key_act), by_head(value_act), by_head(d_attn)))
    normed = back(normed)
    grad_weight = jnp.dot(out_cotangent.T, normed, preferred_element_type=jnp.float32) * (1.0 / jnp.sqrt(jnp.float32(TOKENS)))
    return (back(grad_q), back(grad_k), back(grad_v), grad_weight)
```

```python
import functools
import math

import jax
import jax.numpy as jnp
from jax import lax
from jax.experimental import pallas as pl
from jax.experimental.pallas import tpu as pltpu
from jax.sharding import PartitionSpec as P

HDIM = 128
BLK = 256


EPS = 1e-06


def carried_in(part, axis, combine, identity):
    place = lax.axis_index(axis)
    gathered = lax.all_gather(part, axis)
    state = jnp.zeros_like(part) + jnp.asarray(identity, part.dtype)

    def carried_one(lap, state):
        return combine(state, lax.dynamic_index_in_dim(gathered, lap, 0, False))

    return lax.fori_loop(0, place, carried_one, state)


def prefix(x, axis, join, neutral):
    count = lax.axis_size(axis)
    place = lax.axis_index(axis)
    ahead = count - 1 - place
    gathered = lax.all_gather(x.astype(jnp.bfloat16), axis)
    state = jnp.zeros_like(x) + jnp.asarray(neutral, x.dtype)

    def prefix_one(lap, state):
        source = count - 1 - lap
        return join(state, lax.dynamic_index_in_dim(gathered, source, 0, False).astype(x.dtype))

    return lax.fori_loop(0, ahead, prefix_one, state)


def plus(earlier, later_part):
    return earlier + later_part


def general_body(query_act, key_act, value_act, out_weight, out_cotangent):
    tok_rows = query_act.shape[0]
    width = query_act.shape[1]
    heads = width // HDIM
    nb = tok_rows // BLK
    ctx_count = lax.axis_size("ctx")
    scale = 1.0 / math.sqrt(tok_rows * ctx_count)
    cot_full = lax.all_gather(out_cotangent, "head", axis=1, tiled=True)
    d_attn = jnp.dot(
        cot_full,
        lax.all_gather(out_weight, "ctx", axis=0, tiled=True),
        preferred_element_type=jnp.float32,
    )
    shape4 = (nb, BLK, heads, HDIM)
    q4 = query_act.reshape(shape4)
    k4 = key_act.reshape(shape4)
    v4 = value_act.reshape(shape4)
    block_kv = jnp.einsum("bthi,bthj->bhij", k4, v4, preferred_element_type=jnp.float32)
    shard_kv = jnp.sum(block_kv, axis=0)
    zeros_state = jnp.zeros_like(shard_kv)
    incoming = carried_in(shard_kv, "ctx", plus, zeros_state)
    prior = (incoming[None] + jnp.cumsum(block_kv, axis=0) - block_kv).astype(jnp.bfloat16)
    mask = jnp.tril(jnp.ones((BLK, BLK), jnp.float32))
    scores = (
        jnp.einsum("bthi,bshi->bhts", q4, k4, preferred_element_type=jnp.float32) * mask
    ).astype(jnp.bfloat16)
    raw = jnp.einsum("bhts,bshj->bthj", scores, v4, preferred_element_type=jnp.float32)
    raw = raw + jnp.einsum("bthi,bhij->bthj", q4, prior, preferred_element_type=jnp.float32)
    inv_rms = lax.rsqrt(jnp.mean(raw * raw, axis=-1, keepdims=True) + EPS)
    normal = raw * inv_rms
    normed = normal.astype(jnp.bfloat16).reshape(tok_rows, width)
    d_in = d_attn.reshape(shape4)
    center = jnp.mean(d_in * normal, axis=-1, keepdims=True)
    d_raw = (inv_rms * (d_in - normal * center)).astype(jnp.bfloat16)
    block_g = jnp.einsum("bthi,bthj->bhij", q4, d_raw, preferred_element_type=jnp.float32)
    shard_g = jnp.sum(block_g, axis=0)
    incoming_g = prefix(shard_g, "ctx", plus, zeros_state)
    later = (incoming_g[None] + shard_g[None] - jnp.cumsum(block_g, axis=0)).astype(jnp.bfloat16)
    d_scores = (
        jnp.einsum("bthj,bshj->bhts", d_raw, v4, preferred_element_type=jnp.float32) * mask
    ).astype(jnp.bfloat16)
    grad_q = jnp.einsum("bhts,bshi->bthi", d_scores, k4, preferred_element_type=jnp.float32)
    grad_q = grad_q + jnp.einsum(
        "bthj,bhij->bthi", d_raw, prior, preferred_element_type=jnp.float32
    )
    grad_k = jnp.einsum("bhts,bthi->bshi", d_scores, q4, preferred_element_type=jnp.float32)
    grad_k = grad_k + jnp.einsum("bshj,bhij->bshi", v4, later, preferred_element_type=jnp.float32)
    grad_v = jnp.einsum("bhts,bthj->bshj", scores, d_raw, preferred_element_type=jnp.float32)
    grad_v = grad_v + jnp.einsum("bshi,bhij->bshj", k4, later, preferred_element_type=jnp.float32)
    contract = (((0,), (0,)), ((), ()))
    my_columns = lax.all_to_all(cot_full, "ctx", split_axis=1, concat_axis=0, tiled=True)
    grad_weight = (
        lax.dot_general(
            my_columns,
            lax.all_gather(normed, "ctx", axis=0, tiled=True),
            contract,
            preferred_element_type=jnp.float32,
        )
        * scale
    )
    return (
        grad_q.reshape(tok_rows, width).astype(jnp.bfloat16),
        grad_k.reshape(tok_rows, width).astype(jnp.bfloat16),
        grad_v.reshape(tok_rows, width).astype(jnp.bfloat16),
        grad_weight,
    )


AXES = ("ctx", "head")
f32 = jnp.float32
bf16 = jnp.bfloat16


def mm(a, b, ca, cb):
    return lax.dot_general(a, b, (((ca,), (cb,)), ((), ())), preferred_element_type=f32)


def lower_mask():
    rows = lax.broadcasted_iota(jnp.int32, (BLK, BLK), 0)
    cols = lax.broadcasted_iota(jnp.int32, (BLK, BLK), 1)
    return cols <= rows


def kv_kernel(k_ref, v_ref, kv_ref):
    kv_ref[...] = mm(k_ref[...], v_ref[...], 0, 0).astype(bf16)


def forward_kernel(q_ref, k_ref, v_ref, prior_ref, raw_ref, scores_ref, normed_ref):
    q, v = q_ref[...], v_ref[...]
    scores = jnp.where(lower_mask(), mm(q, k_ref[...], 1, 1), 0.0).astype(bf16)
    raw = mm(scores, v, 1, 0) + mm(q, prior_ref[...], 1, 0)
    inv_rms = lax.rsqrt(jnp.mean(raw * raw, axis=-1, keepdims=True) + EPS)
    raw_ref[...] = raw
    scores_ref[...] = scores
    normed_ref[...] = (raw * inv_rms).astype(bf16)


def backward_kernel(
    q_ref, k_ref, v_ref, prior_ref, raw_ref, scores_ref, da_ref,
    g_ref, gq_ref, gk_ref, gv_ref,
):
    q, k, v = q_ref[...], k_ref[...], v_ref[...]
    raw, da = raw_ref[...], da_ref[...].astype(f32)
    inv_rms = lax.rsqrt(jnp.mean(raw * raw, axis=-1, keepdims=True) + EPS)
    a = raw * inv_rms
    center = jnp.mean(da * a, axis=-1, keepdims=True)
    d_raw = (inv_rms * (da - a * center)).astype(bf16)
    g_ref[...] = mm(q, d_raw, 0, 0).astype(bf16)
    d_scores = jnp.where(lower_mask(), mm(d_raw, v, 1, 1), 0.0).astype(bf16)
    gq = mm(d_scores, k, 1, 0) + mm(d_raw, prior_ref[...], 1, 1)
    gq_ref[...] = gq.astype(bf16)
    gk_ref[...] = mm(d_scores, q, 0, 0)
    gv_ref[...] = mm(scores_ref[...], d_raw, 0, 0)


def finish_kernel(k_ref, v_ref, later_ref, gk_in_ref, gv_in_ref, gk_ref, gv_ref):
    later = later_ref[...]
    gk_ref[...] = (gk_in_ref[...] + mm(v_ref[...], later, 1, 1)).astype(bf16)
    gv_ref[...] = (gv_in_ref[...] + mm(k_ref[...], later, 1, 0)).astype(bf16)


def per_head(kernel, heads, inputs, outputs, flops):
    token = pl.BlockSpec((BLK, HDIM), lambda h: (0, h))
    state = pl.BlockSpec((HDIM, HDIM), lambda h: (h, 0))
    square = pl.BlockSpec((BLK, BLK), lambda h: (h, 0))
    kinds = {"token": token, "state": state, "square": square}
    shapes = {
        "token": (BLK, heads * HDIM),
        "state": (heads * HDIM, HDIM),
        "square": (heads * BLK, BLK),
    }
    moved = sum(x.size * x.dtype.itemsize for _, x in inputs)
    return pl.pallas_call(
        kernel,
        grid=(heads,),
        in_specs=[kinds[kind] for kind, _ in inputs],
        out_specs=[kinds[kind] for kind, _ in outputs],
        out_shape=[jax.ShapeDtypeStruct(shapes[kind], dtype) for kind, dtype in outputs],
        cost_estimate=pl.CostEstimate(
            flops=flops * heads, bytes_accessed=2 * moved, transcendentals=0
        ),
    )(*[x for _, x in inputs])


def fast_body(ctx_count, head_count, query_act, key_act, value_act, out_weight, out_cotangent):
    tok_rows, width = query_act.shape
    heads = width // HDIM
    rows = out_weight.shape[0]
    groups = ctx_count // 2
    halves = head_count // 2
    scale = 1.0 / math.sqrt(tok_rows * ctx_count)
    c = lax.axis_index("ctx")
    hd = lax.axis_index("head")
    z, y = c >> 1, c & 1
    x, k = hd >> 1, hd & 1

    def send(value, to):
        pairs = []
        for z0 in range(groups):
            for y0 in range(2):
                for x0 in range(halves):
                    for k0 in range(2):
                        z1, y1, x1, k1 = to(z0, y0, x0, k0)
                        source = (2 * z0 + y0) * head_count + 2 * x0 + k0
                        pairs.append((source, (2 * z1 + y1) * head_count + 2 * x1 + k1))
        return lax.ppermute(value, AXES, pairs)

    def swapped(value):
        return send(value, lambda z, y, x, k: (z, k, x, y))

    def across(value, bit):
        return send(value, lambda z, y, x, k: (z ^ bit, y, x, k))

    def scanned(total, after):
        found = jnp.zeros(total.shape, f32)
        for bit in range(ctx_count.bit_length() - 1):
            def partner(z, y, x, k, bit=bit):
                other = (2 * z + y) ^ (1 << bit)
                return other // 2, other % 2, x, k
            got = send(total, partner).astype(f32)
            mine = (c >> bit) & 1
            found = found + jnp.where(mine == (0 if after else 1), got, 0.0)
            total = (total.astype(f32) + got).astype(bf16)
        return found.astype(bf16)

    (kv,) = per_head(
        kv_kernel, heads, [("token", key_act), ("token", value_act)], [("state", bf16)],
        2 * BLK * HDIM * HDIM,
    )
    first = send(
        out_cotangent,
        lambda z, y, x, k: (2 * x + k, z % 2, (z // 2) ^ k, y),
    )
    over_x = send(first, lambda z, y, x, k: (z, y, x ^ 1, k))
    over_y = send(first, lambda z, y, x, k: (z, 1 - y, x, k))
    over_xy = send(first, lambda z, y, x, k: (z, 1 - y, x ^ 1, k))
    weight_own = swapped(out_weight)
    weight_other = send(weight_own, lambda z, y, x, k: (z, y, x, 1 - k))
    prior = scanned(kv, False)
    raw, scores, normed = per_head(
        forward_kernel, heads,
        [("token", query_act), ("token", key_act), ("token", value_act), ("state", prior)],
        [("token", f32), ("square", bf16), ("token", bf16)],
        2 * BLK * HDIM * (2 * BLK + HDIM),
    )
    held = (2 * (x ^ (z & 1)) + y) ^ z
    stack = jnp.zeros((groups, tok_rows, 2, rows), bf16)
    for position, part in enumerate((first, over_y, over_x, over_xy)):
        stack = lax.dynamic_update_slice(
            stack, part.reshape(1, tok_rows, 2, rows), (position ^ held, 0, 0, 0)
        )
    cot_own = lax.dynamic_index_in_dim(stack, k, 2, False)
    cot_other = lax.dynamic_index_in_dim(stack, 1 - k, 2, False)

    def partial(step):
        return mm(cot_own[step], weight_own, 1, 0) + mm(cot_other[step], weight_other, 1, 0)

    near_far = across(partial(3).astype(bf16), 1)
    near_own = across(partial(1).astype(bf16), 1)
    far = across((partial(2) + near_far.astype(f32)).astype(bf16), 2)
    d_attn = partial(0) + near_own.astype(f32) + far.astype(f32)
    d_attn = swapped(d_attn.astype(bf16))
    g, grad_q, gk_local, gv_local = per_head(
        backward_kernel, heads,
        [
            ("token", query_act), ("token", key_act), ("token", value_act),
            ("state", prior), ("token", raw), ("square", scores), ("token", d_attn),
        ],
        [("state", bf16), ("token", bf16), ("token", f32), ("token", f32)],
        2 * BLK * HDIM * (4 * BLK + 2 * HDIM),
    )
    later = scanned(g, True)
    grad_k, grad_v = per_head(
        finish_kernel, heads,
        [
            ("token", key_act), ("token", value_act), ("state", later),
            ("token", gk_local), ("token", gv_local),
        ],
        [("token", bf16), ("token", bf16)],
        4 * BLK * HDIM * HDIM,
    )
    n0 = swapped(normed)
    n2 = across(n0, 2)
    n1 = across(n0, 1)
    n3 = across(n2, 1)
    all_n = (n0, n1, n2, n3)

    def weight_part(cot):
        return sum(mm(cot[step], all_n[step], 0, 0) for step in (0, 2, 1, 3))

    sent = send(weight_part(cot_other).astype(bf16), lambda z, y, x, k: (z, y, x, 1 - k))
    total = (weight_part(cot_own) + sent.astype(f32)) * scale
    grad_weight = swapped(total.astype(bf16)).astype(f32)
    return grad_q, grad_k, grad_v, grad_weight


def solution(mesh):
    ctx_count, head_count = mesh.shape["ctx"], mesh.shape["head"]
    placed = P("ctx", "head")

    def body(query_act, *others):
        if ctx_count == 2 * head_count and head_count == 4 and query_act.shape[0] == BLK:
            return fast_body(ctx_count, head_count, query_act, *others)
        return general_body(query_act, *others)

    return jax.shard_map(
        body,
        mesh=mesh,
        in_specs=(placed,) * 5,
        out_specs=(placed,) * 4,
        check_vma=False,
    )
```
